512 devices in a mesh: row: 32 (over z_lo, y), col: 16 (over z_hi, x, core).
Axes of the slice: x: 4, y: 8, z: 8 (z_hi: 2, z_lo: 4; z = z_hi * 4 + z_lo), core: 2. Of those that a mesh axis runs over, the one named last changes fastest.
Arguments:
- tiles: bfloat16 [16384, 2, 8192], P('row', None, 'col'), may hold values from -0.078125 to 0.078125
- energy: float32 [16384], P(('row', 'col')), may hold values from 0.5 to 8
- vectors: float32 [16, 16384], P(None, ('row', 'col')), may hold values from -6 to 6
- previous: float32 [16, 16384], P(None, ('row', 'col')), may hold values from -6 to 6
- coefs: float32 [2, 3, 16, 16], replicated, may hold values from -0.875 to 0.875
- irrep_of_unit: int32 [256], replicated, may hold values from 0 to 63, never falling along the last dimension, each value on 1 to 8 neighbouring positions
- coupled: int32 [64, 64], replicated, may hold values 0 or 1
Outputs:
- field: float32 [16, 16384], P(None, ('row', 'col'))
- search: float32 [16, 16384], P(None, ('row', 'col'))
- thetas: float32 [2, 16], replicated
The draws below stay inside these ranges and needn't reach their ends.
Inputs may be any that keep to these rules, and one draw needn't show every extreme that they name: `irrep_of_unit`: never falls along the units; each irrep is a run of 1 to 8 units, and some irrep has exactly 8.
All inputs are finite; a program needn't handle non-finite values.
Results may differ from the reference program's by a relative error of at most 0.0011.
Values may be sent and summed in bfloat16 or wider, within the bound.
A program may use at most 64 MiB of HBM per device.

```python
import math
import jax
import jax.numpy as jnp
import numpy as np
from jax import lax

SEG = 512
NVEC = 16
ITERS = 2
UNIT = 64
ORDER = 16384
UNITS = 256
IRREPS = 64
N_ROW = 32
N_COL = 16


def plant(array, own_key, smallest, largest):
    extent = array.shape
    index_at = [jax.random.randint(jax.random.fold_in(own_key, axis), (), 0, extent[axis]) for axis in range(len(extent))]
    array = array.at[tuple(index_at)].set(smallest)
    longest = extent.index(max(extent))
    index_at[longest] = (index_at[longest] + 1) % extent[longest]
    return array.at[tuple(index_at)].set(largest)


def level_of(rng, shape, pieces, least, top_value):
    loudness = 1.0
    for dim, parts in pieces:
        draws = jax.random.uniform(jax.random.fold_in(jax.random.fold_in(rng, 6), dim), (parts,), jnp.float32, least / len(pieces), top_value / len(pieces))
        loudness = loudness * jnp.repeat(jnp.exp(draws), shape[dim] // parts).reshape((-1,) + (1,) * (len(shape) - 1 - dim))
    return loudness


def profile(number_of, total, most, slope):
    weights = [(1 << 20) // math.isqrt(grade ** slope) + 1 for grade in range(2, number_of + 1)]
    rest, counts = total - most - (number_of - 1), [1] * (number_of - 1)
    while rest > 0:
        movable = [i for i in range(number_of - 1) if counts[i] < most]
        mass, remaining = sum([weights[i] for i in movable]), rest
        for i in movable:
            more = min(most - counts[i], max(1, remaining * weights[i] // mass), rest)
            counts[i] = counts[i] + more
            rest = rest - more
    return np.array([most] + counts)


def uneven_parts(own_key, count, total, reach, skew):
    if count == 2:
        one = jax.random.randint(own_key, (), max(1, total - reach), min(reach, total - 1) + 1)
        return jnp.stack([one, total - one])
    tallies = jnp.asarray(profile(count, total, reach, skew), jnp.int32)
    twos = (count - 1) // 2
    giver, sink = tallies[1:1 + 2 * twos:2], tallies[2:2 + 2 * twos:2]
    margin = jnp.minimum(giver - 1, reach - sink)
    passed = jax.random.randint(jax.random.fold_in(own_key, 1), (twos,), 0, 1 << 20) % (margin + 1)
    tallies = tallies.at[1:1 + 2 * twos:2].set(giver - passed).at[2:2 + 2 * twos:2].set(sink + passed)
    return tallies[jax.random.permutation(jax.random.fold_in(own_key, 2), count)]


def centred(key, shape, scale, reach, shards=(), kind=jnp.bfloat16):
    drawn = jax.random.normal(key, shape, jnp.float32) * scale
    if len(shards) > 0:
        drawn = level_of(key, shape, shards, -0.22, 0.18) * drawn
    return jnp.clip(drawn, min=-reach, max=reach).astype(kind)


def setup_inputs(seed: int = 0) -> dict:
    keys = jax.random.split(jax.random.key(seed), 8)
    tiles = centred(keys[0], (ORDER, 2, N_COL * SEG), (ORDER // 3) ** -0.5, 0.078125, ((0, 32), (2, 16)))
    energy = jnp.clip(jnp.exp(math.log(8.0) - 2.7725887 * jax.random.uniform(keys[1], (ORDER,), jnp.float32) ** level_of(keys[1], (ORDER,), ((0, 512),), -0.2, 0.2)), 0.5, 8.0)
    vectors = centred(keys[2], (NVEC, ORDER), 1.0, 6.0, ((1, 512),), jnp.float32)
    previous = centred(keys[3], (NVEC, ORDER), 1.0, 6.0, ((1, 512),), jnp.float32)
    coefs = centred(keys[4], (ITERS, 3, NVEC, NVEC), (3 * NVEC) ** -0.5, 0.875, (), jnp.float32)
    irrep_of_unit = jnp.searchsorted(jnp.cumsum(uneven_parts(keys[5], IRREPS, UNITS, 8, 2)), jnp.arange(UNITS), side="right").astype(jnp.int32)
    coupled = plant((jax.random.randint(keys[6], (IRREPS, IRREPS), 0, 3) < 1).astype(jnp.int32), jax.random.fold_in(keys[6], 1), 0, 1)
    return dict(tiles=tiles, energy=energy, vectors=vectors, previous=previous, coefs=coefs, irrep_of_unit=irrep_of_unit, coupled=coupled)


def reference(tiles, energy, vectors, previous, coefs, irrep_of_unit, coupled):
    order = N_ROW * SEG
    seg_units = SEG // UNIT
    all_units = order // UNIT
    col_index = jnp.arange(order, dtype=jnp.int32)

    def masked_rows(block):
        start = (block * SEG).astype(jnp.int32)
        rows = lax.dynamic_slice_in_dim(tiles, start, SEG, 0).reshape(SEG, order)
        row_ids = lax.dynamic_slice_in_dim(irrep_of_unit, (block * seg_units).astype(jnp.int32), seg_units, 0)
        unit_mask = coupled[row_ids][:, irrep_of_unit]
        full = jnp.broadcast_to(unit_mask[:, None, :, None], (seg_units, UNIT, all_units, UNIT)).reshape(SEG, order)
        row_index = start + jnp.arange(SEG, dtype=jnp.int32)
        keep = (full > 0) & (col_index[None, :] <= row_index[:, None])
        return jnp.where(keep, rows, jnp.zeros_like(rows))

    def apply_ham(current):
        narrow = current.astype(jnp.bfloat16)

        def step(total, block):
            part = masked_rows(block)
            seg_vec = lax.dynamic_slice_in_dim(narrow, (block * SEG).astype(jnp.int32), SEG, 1)
            direct = jnp.dot(narrow, part.T, preferred_element_type=jnp.float32)
            total = total + jnp.dot(seg_vec, part, preferred_element_type=jnp.float32)
            return (total, direct)
        total, direct = lax.scan(step, jnp.zeros((NVEC, order), jnp.float32), jnp.arange(N_ROW, dtype=jnp.int32))
        direct = jnp.transpose(direct, (1, 0, 2)).reshape(NVEC, order)
        return direct + total + energy[None, :] * current
    field = vectors
    search = previous
    quotients = []
    high = lax.Precision.HIGHEST
    for iteration in range(ITERS):
        image = apply_ham(field)
        self_dot = lax.optimization_barrier(jnp.sum(field * field, axis=1))
        cross = lax.optimization_barrier(jnp.sum(field * image, axis=1))
        theta = cross / self_dot
        resid = image - theta[:, None] * field
        spread = lax.optimization_barrier(jnp.sum(resid * resid, axis=1))
        scaled = resid * lax.rsqrt(spread / order + 1e-06)[:, None]
        new_search = jnp.dot(coefs[iteration, 1].T, scaled, precision=high) + jnp.dot(coefs[iteration, 2].T, search, precision=high)
        field = jnp.dot(coefs[iteration, 0].T, field, precision=high) + new_search
        search = new_search
        quotients.append(theta)
    return (field, search, jnp.stack(quotients))
```

```python
import jax
import jax.numpy as jnp
from jax import lax
from jax.experimental import pallas as pl
from jax.experimental.pallas import tpu as pltpu
from jax.sharding import PartitionSpec as P

MESH = pl.DeviceIdType.MESH
UNIT = 64
ROWS = 32
COLS = 16
SEG = 512
NVEC = 16
LANES = 128
GROUP = 4
TINY = 1e-37


def remote(src, dst, send, recv, row, col):
    return pltpu.make_async_remote_copy(
        src_ref=src, dst_ref=dst, send_sem=send, recv_sem=recv, device_id=(row, col), device_id_type=MESH
    )


def wait_all(ref, sem):
    pltpu.make_async_copy(ref, ref, sem).wait()


def segment_of(ref):
    tiles = []
    for t in range(SEG // LANES):
        tiles.append(jnp.concatenate([ref[4 * t + g] for g in range(GROUP)], axis=0))
    return jnp.concatenate(tiles, axis=1)


def store_pieces(ref, value):
    for t in range(value.shape[1] // LANES):
        for g in range(GROUP):
            ref[4 * t + g] = value[4 * g : 4 * g + 4, LANES * t : LANES * (t + 1)]


def mixed(mix, field, scaled, search):
    rest = jnp.zeros((LANES - 3 * NVEC, field.shape[1]), jnp.float32)
    stack = jnp.concatenate([field, scaled, search, rest], axis=0)
    return jnp.dot(mix, stack, precision=lax.Precision.HIGHEST, preferred_element_type=jnp.float32)


def kernel(
    own_ref, masked_ref, mix_ref,
    field_out, search_out, theta_out,
    group_buf, field_piece, search_piece, next_piece,
    field_row, field_col, search_row, search_col, image_row, image_col, last_row,
    direct_out, mirror_out, sums, sums_next, image_piece, image_next,
    stat_out, stats, stats_next, field_next,
    group_send, group_recv,
    field_send, field_recv, search_send, search_recv, image_send, image_recv, last_send, last_recv,
    sums_send, sums_recv, stat_send, stat_recv,
):
    row = lax.axis_index("row")
    col = lax.axis_index("col")
    tile = col // GROUP
    lane_group = col % GROUP
    home = lax.rem(row, COLS)
    half = row // COLS
    on_diag = home == col
    depth = (col // 8) * 4 + row // 8
    inner = lax.rem(col, 8)

    def stat_peer(index, sign):
        step = (index // 8 - 1) * sign
        there = lax.rem(depth + step + 8, 8)
        return lax.rem(there, 4) * 8 + lax.rem(index, 8), (there // 4) * 8 + inner

    def is_self(r, c):
        return jnp.logical_and(r == row, c == col)

    barrier = pltpu.get_barrier_semaphore()

    def greet(r, c):
        @pl.when(jnp.logical_not(is_self(r, c)))
        def _():
            pl.semaphore_signal(barrier, inc=1, device_id=(r, c), device_id_type=MESH)

    def greet_32(k, carry):
        greet(k, home)
        greet(lax.rem(k, 2) * COLS + col, k // 2)
        greet(*stat_peer(k, -1))
        return carry

    def greet_16(k, carry):
        greet(row, k)
        return carry

    lax.fori_loop(0, ROWS, greet_32, 0)
    lax.fori_loop(0, COLS, greet_16, 0)
    pl.semaphore_wait(barrier, 15 + 31 + 64 - 2 * on_diag.astype(jnp.int32))

    def put(src, dst, send, recv, r, c):
        mine = is_self(r, c)

        @pl.when(jnp.logical_not(mine))
        def _():
            remote(src, dst, send, recv, r, c).start()

        @pl.when(mine)
        def _():
            pltpu.make_async_copy(src, dst, recv).start()

    def group_put(k, carry):
        put(own_ref, group_buf.at[lane_group], group_send, group_recv, row, GROUP * tile + k)
        return carry

    lax.fori_loop(0, GROUP, group_put, 0)
    wait_all(group_buf, group_recv)
    own = (group_buf[0] + group_buf[1]) + (group_buf[2] + group_buf[3])
    field_t = own[0:16]
    search_t = own[16:32]
    energy = own[32:33]
    store_pieces(field_piece, field_t)
    store_pieces(search_piece, search_t)

    def row_put(src, dst, send, recv):
        def step(k, carry):
            put(src, dst.at[col], send, recv, row, k)
            return carry

        lax.fori_loop(0, COLS, step, 0)

    def col_put(src, dst, send, recv):
        def step(k, carry):
            put(src, dst.at[half, col], send, recv, lax.rem(row + k, ROWS), home)
            return carry

        lax.fori_loop(0, ROWS, step, 0)

    col_put(field_piece.at[lane_group], field_col, field_send.at[0], field_recv.at[0])
    row_put(field_piece.at[lane_group], field_row, field_send.at[1], field_recv.at[1])
    col_put(search_piece.at[lane_group], search_col, search_send.at[0], search_recv.at[0])
    row_put(search_piece.at[lane_group], search_row, search_send.at[1], search_recv.at[1])

    def multiply(narrow_row, narrow_cols, out_sums, which):
        direct = jnp.zeros((NVEC, SEG), jnp.float32)
        for h in range(2):
            block = masked_ref[h]
            mirror = jnp.dot(narrow_row, block, preferred_element_type=jnp.float32)
            store_pieces(mirror_out.at[which, h], mirror)
            direct = direct + lax.dot_general(
                narrow_cols[h], block, (((1,), (1,)), ((), ())), preferred_element_type=jnp.float32
            )
        store_pieces(direct_out.at[which], direct)

        def mirror_put(k, carry):
            h = k // COLS
            j = lax.rem(k, COLS)
            put(mirror_out.at[which, h, j], out_sums.at[COLS + row], sums_send.at[which, 0], sums_recv.at[which], COLS * h + col, j)
            return carry

        def direct_put(k, carry):
            put(direct_out.at[which, k], out_sums.at[col], sums_send.at[which, 1], sums_recv.at[which], row, k)
            return carry

        lax.fori_loop(0, 2 * COLS, mirror_put, 0)
        lax.fori_loop(0, COLS, direct_put, 0)

    sub = lax.broadcasted_iota(jnp.int32, (NVEC, LANES), 0)
    lane = lax.broadcasted_iota(jnp.int32, (NVEC, LANES), 1)
    eye = sub == lane

    def to_lanes(column):
        return jnp.sum(jnp.where(eye, column, 0.0), axis=0, keepdims=True)

    def to_column(lanes):
        return jnp.sum(jnp.where(eye, lanes, 0.0), axis=1, keepdims=True)

    def share_stats(field, image, dst, which):
        self_dot = jnp.sum(field * field, axis=1, keepdims=True)
        cross = jnp.sum(field * image, axis=1, keepdims=True)
        usable = self_dot > TINY
        local = jnp.where(usable, cross / jnp.where(usable, self_dot, 1.0), 0.0)
        left = image - local * field
        spread = jnp.sum(left * left, axis=1, keepdims=True)
        for i, value in enumerate((self_dot, cross, spread, local)):
            stat_out[which, i : i + 1, :] = to_lanes(value)

        def step(k, carry):
            r, c = stat_peer(k, 1)
            put(stat_out.at[which], dst.at[row], stat_send.at[which], stat_recv.at[which], r, c)
            return carry

        lax.fori_loop(0, ROWS, step, 0)

    def merge_stats(src, which):
        wait_all(src, stat_recv.at[which])
        self_i, cross_i, spread_i, local_i = [src[:, i, :] for i in range(4)]
        self_dot = jnp.sum(self_i, axis=0, keepdims=True)
        cross = jnp.sum(cross_i, axis=0, keepdims=True)
        theta = cross / jnp.where(lane[0:1] < NVEC, self_dot, 1.0)
        away = local_i - theta
        spread = jnp.sum(spread_i + self_i * away * away, axis=0, keepdims=True)
        scale = lax.rsqrt(spread / (ROWS * SEG) + 1e-06)
        theta_out[which : which + 1, :] = theta[:, :NVEC]
        return to_column(theta), to_column(scale)

    wait_all(field_row, field_recv.at[1])
    field_r = segment_of(field_row)
    wait_all(field_col, field_recv.at[0])
    field_c = [segment_of(field_col.at[h]) for h in range(2)]
    multiply(field_r.astype(jnp.bfloat16), [x.astype(jnp.bfloat16) for x in field_c], sums, 0)

    wait_all(search_row, search_recv.at[1])
    wait_all(search_col, search_recv.at[0])
    wait_all(sums, sums_recv.at[0])
    image_piece[...] = jnp.sum(sums[...], axis=0) + energy * field_piece[lane_group]
    row_put(image_piece, image_row, image_send.at[1], image_recv.at[1])
    col_put(image_piece, image_col, image_send.at[0], image_recv.at[0])
    wait_all(image_row, image_recv.at[1])
    field_r = segment_of(field_row)
    image_r = segment_of(image_row)
    share_stats(field_r, image_r, stats, 0)
    wait_all(image_col, image_recv.at[0])
    theta, scale = merge_stats(stats, 0)

    images = [image_r] + [segment_of(image_col.at[h]) for h in range(2)]
    fields = [field_r] + [segment_of(field_col.at[h]) for h in range(2)]
    searches = [segment_of(search_row)] + [segment_of(search_col.at[h]) for h in range(2)]
    narrow = []
    for i in range(3):
        scaled = (images[i] - theta * fields[i]) * scale
        following = mixed(mix_ref[0, 0:NVEC], fields[i], scaled, searches[i])
        if i == 0:
            field_next[...] = following
        narrow.append(following.astype(jnp.bfloat16))
    multiply(narrow[0], narrow[1:], sums_next, 1)
    image_t = jnp.concatenate([image_row[GROUP * tile + g] for g in range(GROUP)], axis=0)
    scaled_t = (image_t - theta * field_t) * scale
    both = mixed(mix_ref[0], field_t, scaled_t, search_t)
    field_t, search_t = both[0:NVEC], both[NVEC:]
    store_pieces(next_piece, field_t)

    wait_all(sums_next, sums_recv.at[1])
    image_next[...] = jnp.sum(sums_next[...], axis=0) + energy * next_piece[lane_group]
    row_put(image_next, last_row, last_send, last_recv)
    wait_all(last_row, last_recv)
    share_stats(field_next[...], segment_of(last_row), stats_next, 1)
    theta, scale = merge_stats(stats_next, 1)
    image_t = jnp.concatenate([last_row[GROUP * tile + g] for g in range(GROUP)], axis=0)
    scaled_t = (image_t - theta * field_t) * scale
    both = mixed(mix_ref[1], field_t, scaled_t, search_t)
    field_t, search_t = both[0:NVEC], both[NVEC:]
    shift = lax.rem(LANES - (LANES // GROUP) * lane_group, LANES)
    field_out[...] = pltpu.roll(field_t, shift, 1)[:, : LANES // GROUP]
    search_out[...] = pltpu.roll(search_t, shift, 1)[:, : LANES // GROUP]

    wait_all(group_buf.at[pl.ds(0, GROUP - 1)], group_send)

    def drain(sem, ref, whole, diagonal):
        if not diagonal:
            wait_all(ref.at[pl.ds(0, whole)], sem)
        else:
            @pl.when(on_diag)
            def _():
                wait_all(ref.at[pl.ds(0, whole - 1)], sem)

            @pl.when(jnp.logical_not(on_diag))
            def _():
                wait_all(ref.at[pl.ds(0, whole)], sem)

    for sem in (field_send, search_send, image_send):
        drain(sem.at[0], sums, ROWS, True)
        drain(sem.at[1], sums, COLS - 1, False)
    drain(last_send, sums, COLS - 1, False)
    for which in range(2):
        drain(sums_send.at[which, 0], sums, 2 * COLS, True)
        drain(sums_send.at[which, 1], sums, COLS - 1, False)
        drain(stat_send.at[which], sums, ROWS - 1, False)


def body(tiles, energy, vectors, previous, coefs, irrep_of_unit, coupled):
    grid_row = lax.axis_index("row")
    grid_col = lax.axis_index("col")
    seg_units = SEG // UNIT
    labels = jnp.arange(coupled.shape[0], dtype=jnp.int32)
    row_ids = lax.dynamic_slice_in_dim(irrep_of_unit, grid_row * seg_units, seg_units, 0)
    row_hot = (row_ids[:, None] == labels[None, :]).astype(jnp.float32)
    row_couple = jnp.dot(row_hot, coupled.astype(jnp.float32))
    rows_global = grid_row * SEG + jnp.arange(SEG, dtype=jnp.int32)
    masked_list = []
    for which_half in range(2):
        block_index = which_half * COLS + grid_col
        col_ids = lax.dynamic_slice_in_dim(irrep_of_unit, block_index * seg_units, seg_units, 0)
        col_hot = (col_ids[:, None] == labels[None, :]).astype(jnp.float32)
        unit_mask = jnp.dot(row_couple, col_hot.T)
        full_mask = jnp.broadcast_to(
            unit_mask[:, None, :, None], (seg_units, UNIT, seg_units, UNIT)
        ).reshape(SEG, SEG)
        cols_global = block_index * SEG + jnp.arange(SEG, dtype=jnp.int32)
        lower = cols_global[None, :] <= rows_global[:, None]
        keep = jnp.where(lower & (full_mask > 0.5), 1.0, 0.0).astype(jnp.bfloat16)
        masked_list.append(tiles[:, which_half, :] * keep)
    masked = jnp.stack(masked_list)
    mine = jnp.concatenate([vectors, previous, jnp.broadcast_to(energy[None, :], (8, energy.shape[0]))], axis=0)
    place = (jnp.arange(LANES, dtype=jnp.int32) // (LANES // GROUP)) == grid_col % GROUP
    own = jnp.where(place[None, :], jnp.tile(mine, (1, GROUP)), 0.0)
    turned = jnp.swapaxes(coefs, 2, 3)
    search_rows = jnp.concatenate([jnp.zeros_like(turned[:, 0]), turned[:, 1], turned[:, 2]], axis=2)
    field_rows = jnp.concatenate([turned[:, 0], turned[:, 1], turned[:, 2]], axis=2)
    mixes = jnp.concatenate([field_rows, search_rows], axis=1)
    mixes = jnp.pad(mixes, ((0, 0), (0, 0), (0, LANES - 3 * NVEC)))

    f32 = jnp.float32
    dma = pltpu.SemaphoreType.DMA
    vmem = pl.BlockSpec(memory_space=pltpu.VMEM)
    piece = (GROUP, LANES)
    return pl.pallas_call(
        kernel,
        out_shape=(
            jax.ShapeDtypeStruct((NVEC, LANES // GROUP), f32),
            jax.ShapeDtypeStruct((NVEC, LANES // GROUP), f32),
            jax.ShapeDtypeStruct((2, NVEC), f32),
        ),
        in_specs=[vmem] * 3,
        out_specs=(vmem, vmem, vmem),
        scratch_shapes=[
            pltpu.VMEM((GROUP, 40, LANES), f32),
            pltpu.VMEM((GROUP, *piece), f32),
            pltpu.VMEM((GROUP, *piece), f32),
            pltpu.VMEM((GROUP, *piece), f32),
            pltpu.VMEM((COLS, *piece), f32),
            pltpu.VMEM((2, COLS, *piece), f32),
            pltpu.VMEM((COLS, *piece), f32),
            pltpu.VMEM((2, COLS, *piece), f32),
            pltpu.VMEM((COLS, *piece), f32),
            pltpu.VMEM((2, COLS, *piece), f32),
            pltpu.VMEM((COLS, *piece), f32),
            pltpu.VMEM((2, COLS, *piece), f32),
            pltpu.VMEM((2, 2, COLS, *piece), f32),
            pltpu.VMEM((COLS + ROWS, *piece), f32),
            pltpu.VMEM((COLS + ROWS, *piece), f32),
            pltpu.VMEM(piece, f32),
            pltpu.VMEM(piece, f32),
            pltpu.VMEM((2, *piece), f32),
            pltpu.VMEM((ROWS, *piece), f32),
            pltpu.VMEM((ROWS, *piece), f32),
            pltpu.VMEM((NVEC, SEG), f32),
            dma, dma,
            dma((2,)), dma((2,)), dma((2,)), dma((2,)), dma((2,)), dma((2,)), dma, dma,
            dma((2, 2)), dma((2,)), dma((2,)), dma((2,)),
        ],
        compiler_params=pltpu.CompilerParams(collective_id=0, has_side_effects=True),
        name="lobpcg",
    )(own, masked, mixes)


def solution(mesh):
    placed = (
        P("row", None, "col"),
        P(("row", "col")),
        P(None, ("row", "col")),
        P(None, ("row", "col")),
        P(),
        P(),
        P(),
    )
    return jax.shard_map(
        body,
        mesh=mesh,
        in_specs=placed,
        out_specs=(P(None, ("row", "col")), P(None, ("row", "col")), P()),
        check_vma=False,
    )
```

```python
import jax
import jax.numpy as jnp
from jax import lax
from jax.experimental import pallas as pl
from jax.experimental.pallas import tpu as pltpu
from jax.sharding import PartitionSpec as P

MESH = pl.DeviceIdType.MESH
UNIT = 64
ROWS = 32
COLS = 16
SEG = 512
NVEC = 16
LANES = 128
GROUP = 4
QUARTER = LANES // GROUP
TINY = 1e-37


def remote(src, dst, send, recv, row, col):
    return pltpu.make_async_remote_copy(
        src_ref=src, dst_ref=dst, send_sem=send, recv_sem=recv, device_id=(row, col), device_id_type=MESH
    )


def wait_all(ref, sem):
    pltpu.make_async_copy(ref, ref, sem).wait()


def segment_of(ref):
    tiles = []
    for t in range(SEG // LANES):
        tiles.append(jnp.concatenate([ref[4 * t + g] for g in range(GROUP)], axis=0))
    return jnp.concatenate(tiles, axis=1)


def store_pieces(ref, value):
    for t in range(value.shape[1] // LANES):
        for g in range(GROUP):
            ref[4 * t + g] = value[4 * g : 4 * g + 4, LANES * t : LANES * (t + 1)]


def mixed(mix, field, scaled, search):
    rest = jnp.zeros((LANES - 3 * NVEC, field.shape[1]), jnp.float32)
    stack = jnp.concatenate([field, scaled, search, rest], axis=0)
    return jnp.dot(mix, stack, precision=lax.Precision.HIGHEST, preferred_element_type=jnp.float32)


def unpacked(ref):
    block = lax.broadcasted_iota(jnp.int32, (NVEC, LANES), 1) // QUARTER
    rows = []
    for b in range(GROUP):
        total = None
        for g in range(GROUP):
            part = jnp.concatenate([ref[4 * t + g] for t in range(GROUP)], axis=0)
            part = pltpu.roll(part, QUARTER * ((g - b) % GROUP), 1) if g != b else part
            total = part if total is None else jnp.where(block == g, part, total)
        rows.append(total)
    tiles = []
    for t in range(SEG // LANES):
        tiles.append(jnp.concatenate([rows[b][4 * t : 4 * t + 4] for b in range(GROUP)], axis=0))
    return jnp.concatenate(tiles, axis=1)


def kernel(
    tiles_hbm, energy_ref, vectors_ref, previous_ref, coefs_ref, irrep_ref, coupled_ref,
    out_ref,
    tiles_buf, masked, pad, mix_ref, energy_out, energy_buf,
    field_out, search_out, field_piece, next_piece, field_full,
    field_row, field_col, search_row, search_col, image_row, image_col, last_row,
    direct_out, mirror_out, sums, sums_next, image_piece, image_next,
    stat_out, near_stats, far_stats,
    tiles_sem, energy_send, energy_recv,
    field_send, field_recv, search_send, search_recv, image_send, image_recv, last_send, last_recv,
    sums_send, sums_recv, stat_send, stat_recv,
):
    row = lax.axis_index("row")
    col = lax.axis_index("col")
    tile = col // GROUP
    lane_group = lax.rem(col, GROUP)
    home = lax.rem(row, COLS)
    half = row // COLS
    on_diag = home == col
    low = row // 8
    y = lax.rem(row, 8)
    inner = lax.rem(col, 8)
    core = lax.rem(col, 2)
    depth = (col // 8) * 4 + low

    load_tiles = pltpu.make_async_copy(tiles_hbm, tiles_buf, tiles_sem)
    load_tiles.start()

    def near_peer(k):
        z = k // 2
        return lax.rem(z, 4) * 8 + y, (z // 4) * 8 + (inner // 2) * 2 + lax.rem(k, 2)

    def far_peer(k):
        return low * 8 + lax.rem(k, 8), (col // 8) * 8 + (k // 8) * 2 + core

    def is_self(r, c):
        return jnp.logical_and(r == row, c == col)

    barrier = pltpu.get_barrier_semaphore()

    def greet(r, c):
        @pl.when(jnp.logical_not(is_self(r, c)))
        def _():
            pl.semaphore_signal(barrier, inc=1, device_id=(r, c), device_id_type=MESH)

    def greet_sources(k, carry):
        greet(lax.rem(k, 2) * COLS + col, k // 2)
        return carry

    def greet_row(k, carry):
        greet(row, k)
        return carry

    lax.fori_loop(0, ROWS, greet_sources, 0)
    lax.fori_loop(0, COLS, greet_row, 0)

    pad[...] = jnp.zeros_like(pad)
    pad[0:16, 0:QUARTER] = vectors_ref[...]
    pad[16:32, 0:QUARTER] = previous_ref[...]
    pad[32:33, 0:QUARTER] = energy_ref[...]

    def packed(start):
        total = pad[start : start + 4]
        for b in range(1, GROUP):
            total = total + pltpu.roll(pad[start + 4 * b : start + 4 * b + 4], QUARTER * b, 1)
        return total

    field_out[...] = packed(0)
    search_out[...] = packed(16)
    energy_out[...] = pltpu.roll(pad[32:40], QUARTER * lane_group, 1)[0:1]

    pl.semaphore_wait(barrier, 15 + 32 - on_diag.astype(jnp.int32))

    def put(src, dst, send, recv, r, c):
        mine = is_self(r, c)

        @pl.when(jnp.logical_not(mine))
        def _():
            remote(src, dst, send, recv, r, c).start()

        @pl.when(mine)
        def _():
            pltpu.make_async_copy(src, dst, recv).start()

    def row_put(src, dst, send, recv):
        def step(k, carry):
            put(src, dst.at[col], send, recv, row, k)
            return carry

        lax.fori_loop(0, COLS, step, 0)

    def col_put(src, dst, send, recv):
        def step(k, carry):
            put(src, dst.at[half, col], send, recv, lax.rem(row + k, ROWS), home)
            return carry

        lax.fori_loop(0, ROWS, step, 0)

    col_put(field_out, field_col, field_send.at[0], field_recv.at[0])
    row_put(field_out, field_row, field_send.at[1], field_recv.at[1])

    def energy_put(k, carry):
        put(energy_out, energy_buf.at[lane_group], energy_send, energy_recv, row, GROUP * tile + k)
        return carry

    lax.fori_loop(0, GROUP, energy_put, 0)
    col_put(search_out, search_col, search_send.at[0], search_recv.at[0])
    row_put(search_out, search_row, search_send.at[1], search_recv.at[1])

    load_tiles.wait()
    strip_sub = lax.broadcasted_iota(jnp.int32, (UNIT, SEG), 0)
    strip_lane = lax.broadcasted_iota(jnp.int32, (UNIT, SEG), 1)
    unit_lane = lax.broadcasted_iota(jnp.int32, (1, SEG), 1) // UNIT

    def mask_strip(i, carry):
        mine = irrep_ref[row * (SEG // UNIT) + i]
        start = pl.multiple_of(i * UNIT, UNIT)
        for h in range(2):
            block = h * COLS + col
            allowed = jnp.zeros((1, SEG), jnp.int32)
            for j in range(SEG // UNIT):
                theirs = irrep_ref[block * (SEG // UNIT) + j]
                allowed = jnp.where(unit_lane == j, coupled_ref[mine, theirs], allowed)
            lower = strip_lane + block * SEG <= strip_sub + (row * SEG + start)
            keep = jnp.logical_and(lower, allowed > 0)
            strip = tiles_buf[pl.ds(start, UNIT), h, :].astype(jnp.float32)
            masked[h, pl.ds(start, UNIT), :] = jnp.where(keep, strip, 0.0).astype(jnp.bfloat16)
        return carry

    lax.fori_loop(0, SEG // UNIT, mask_strip, 0)

    mix_sub = lax.broadcasted_iota(jnp.int32, (LANES, LANES), 0)
    for i in range(2):
        mix_ref[i] = jnp.zeros((LANES, LANES), jnp.float32)
        for j in range(3):
            mix_ref[i, NVEC * j : NVEC * (j + 1), 0:NVEC] = coefs_ref[i, j]
        square = mix_ref[i]
        square = square + jnp.where(mix_sub >= NVEC, pltpu.roll(square, NVEC, 1), 0.0)
        mix_ref[i] = square.T

    def multiply(narrow_row, narrow_cols, out_sums, which):
        direct = jnp.zeros((NVEC, SEG), jnp.float32)
        for h in range(2):
            block = masked[h]
            mirror = jnp.dot(narrow_row, block, preferred_element_type=jnp.float32)
            store_pieces(mirror_out.at[which, h], mirror)
            direct = direct + lax.dot_general(
                narrow_cols[h], block, (((1,), (1,)), ((), ())), preferred_element_type=jnp.float32
            )
        store_pieces(direct_out.at[which], direct)

        def mirror_put(k, carry):
            h = k // COLS
            j = lax.rem(k, COLS)
            put(mirror_out.at[which, h, j], out_sums.at[COLS + row], sums_send.at[which, 0], sums_recv.at[which], COLS * h + col, j)
            return carry

        def direct_put(k, carry):
            put(direct_out.at[which, k], out_sums.at[col], sums_send.at[which, 1], sums_recv.at[which], row, k)
            return carry

        lax.fori_loop(0, 2 * COLS, mirror_put, 0)
        lax.fori_loop(0, COLS, direct_put, 0)

    sub = lax.broadcasted_iota(jnp.int32, (NVEC, LANES), 0)
    lane = lax.broadcasted_iota(jnp.int32, (NVEC, LANES), 1)
    eye = sub == lane
    eye_group = lane[0:GROUP] == sub[0:GROUP] + GROUP * lane_group

    def to_column(lanes):
        return jnp.sum(jnp.where(eye, lanes, 0.0), axis=1, keepdims=True)

    def quotient(cross, self_dot):
        usable = self_dot > TINY
        return jnp.where(usable, cross / jnp.where(usable, self_dot, 1.0), 0.0)

    def send_stats(rows, which, hop):
        for i, value in enumerate(rows):
            stat_out[which, hop, i : i + 1, :] = value
        src = stat_out.at[which, hop]

        def near_step(k, carry):
            put(src, near_stats.at[which, depth * 2 + core], stat_send.at[which, 0], stat_recv.at[which, 0], *near_peer(k))
            return carry

        def far_step(k, carry):
            put(src, far_stats.at[which, (inner // 2) * 8 + y], stat_send.at[which, 1], stat_recv.at[which, 1], *far_peer(k))
            return carry

        if hop == 0:
            lax.fori_loop(0, COLS, near_step, 0)
        else:
            lax.fori_loop(0, ROWS, far_step, 0)

    def share_stats(field, image, which):
        self_dot = jnp.sum(field * field, axis=1, keepdims=True)
        cross = jnp.sum(field * image, axis=1, keepdims=True)
        local = quotient(cross, self_dot)
        left = image - local * field
        spread = jnp.sum(left * left, axis=1, keepdims=True)
        rows = [
            jnp.sum(jnp.where(eye_group, value, 0.0), axis=0, keepdims=True)
            for value in (self_dot, cross, spread, local)
        ]
        send_stats(rows, which, 0)

    def merged(buf):
        self_i, cross_i, spread_i, local_i = [buf[:, i, :] for i in range(4)]
        self_dot = jnp.sum(self_i, axis=0, keepdims=True)
        cross = jnp.sum(cross_i, axis=0, keepdims=True)
        return self_i, spread_i, local_i, self_dot, cross

    def spread_about(self_i, spread_i, local_i, theta):
        away = local_i - theta
        return jnp.sum(spread_i + self_i * away * away, axis=0, keepdims=True)

    def relay_stats(which):
        buf = near_stats.at[which]
        wait_all(buf, stat_recv.at[which, 0])
        self_i, spread_i, local_i, self_dot, cross = merged(buf)
        local = quotient(cross, self_dot)
        send_stats([self_dot, cross, spread_about(self_i, spread_i, local_i, local), local], which, 1)

    def merge_stats(which):
        buf = far_stats.at[which]
        wait_all(buf, stat_recv.at[which, 1])
        self_i, spread_i, local_i, self_dot, cross = merged(buf)
        theta = cross / jnp.where(lane[0:1] < NVEC, self_dot, 1.0)
        spread = spread_about(self_i, spread_i, local_i, theta)
        scale = lax.rsqrt(spread / (ROWS * SEG) + 1e-06)
        out_ref[48 + which : 49 + which, :] = theta
        return to_column(theta), to_column(scale)

    def tile_of(ref):
        return jnp.concatenate([ref[GROUP * tile + g] for g in range(GROUP)], axis=0)

    def own_tile(ref):
        return ref[:, pl.ds(pl.multiple_of(tile * LANES, LANES), LANES)]

    wait_all(field_row, field_recv.at[1])
    field_r = unpacked(field_row)
    wait_all(field_col, field_recv.at[0])
    field_c = [unpacked(field_col.at[h]) for h in range(2)]
    multiply(field_r.astype(jnp.bfloat16), [x.astype(jnp.bfloat16) for x in field_c], sums, 0)
    fields = [field_r] + field_c
    for i in range(3):
        field_full[0, i] = fields[i]
    field_t = own_tile(field_full.at[0, 0])
    store_pieces(field_piece, field_t)
    wait_all(energy_buf, energy_recv)
    energy = (energy_buf[0] + energy_buf[1]) + (energy_buf[2] + energy_buf[3])
    wait_all(search_row, search_recv.at[1])
    wait_all(search_col, search_recv.at[0])
    searches = [unpacked(search_row)] + [unpacked(search_col.at[h]) for h in range(2)]
    for i in range(3):
        field_full[1, i] = searches[i]
    search_t = own_tile(field_full.at[1, 0])

    wait_all(sums, sums_recv.at[0])
    field_p = field_piece[lane_group]
    image_p = jnp.sum(sums[...], axis=0) + energy * field_p
    image_piece[...] = image_p
    share_stats(field_p, image_p, 0)
    col_put(image_piece, image_col, image_send.at[0], image_recv.at[0])
    row_put(image_piece, image_row, image_send.at[1], image_recv.at[1])
    relay_stats(0)
    wait_all(image_row, image_recv.at[1])
    wait_all(image_col, image_recv.at[0])
    theta, scale = merge_stats(0)

    images = [segment_of(image_row)] + [segment_of(image_col.at[h]) for h in range(2)]
    narrow = []
    for i in range(3):
        field_i = field_full[0, i]
        scaled = (images[i] - theta * field_i) * scale
        following = mixed(mix_ref[0, 0:NVEC], field_i, scaled, field_full[1, i])
        narrow.append(following.astype(jnp.bfloat16))
    multiply(narrow[0], narrow[1:], sums_next, 1)
    scaled_t = (tile_of(image_row) - theta * field_t) * scale
    both = mixed(mix_ref[0, 0 : 2 * NVEC], field_t, scaled_t, search_t)
    field_t, search_t = both[0:NVEC], both[NVEC:]
    store_pieces(next_piece, field_t)
    field_p = next_piece[lane_group]

    wait_all(sums_next, sums_recv.at[1])
    image_p = jnp.sum(sums_next[...], axis=0) + energy * field_p
    image_next[...] = image_p
    share_stats(field_p, image_p, 1)

    def last_put(k, carry):
        put(image_next, last_row.at[lane_group], last_send, last_recv, row, GROUP * tile + k)
        return carry

    lax.fori_loop(0, GROUP, last_put, 0)
    relay_stats(1)
    wait_all(last_row, last_recv)
    theta, scale = merge_stats(1)
    image_t = jnp.concatenate([last_row[g] for g in range(GROUP)], axis=0)
    scaled_t = (image_t - theta * field_t) * scale
    out_ref[0:48, :] = mixed_parts(mix_ref[1, 0 : 2 * NVEC], field_t, scaled_t, search_t, lane_group)

    def drain(sem, ref, whole, diagonal):
        if not diagonal:
            wait_all(ref.at[pl.ds(0, whole)], sem)
        else:
            @pl.when(on_diag)
            def _():
                wait_all(ref.at[pl.ds(0, whole - 1)], sem)

            @pl.when(jnp.logical_not(on_diag))
            def _():
                wait_all(ref.at[pl.ds(0, whole)], sem)

    drain(energy_send, energy_buf, GROUP - 1, False)
    drain(last_send, sums, GROUP - 1, False)
    for sem in (field_send, search_send, image_send):
        drain(sem.at[0], sums, ROWS, True)
        drain(sem.at[1], sums, COLS - 1, False)
    for which in range(2):
        drain(sums_send.at[which, 0], sums, 2 * COLS, True)
        drain(sums_send.at[which, 1], sums, COLS - 1, False)
        drain(stat_send.at[which, 0], sums, COLS - 1, False)
        drain(stat_send.at[which, 1], sums, ROWS - 1, False)


def mixed_parts(mix, field, scaled, search, lane_group):
    both = mixed(mix, field, scaled, search)
    both = pltpu.roll(both, lax.rem(LANES - QUARTER * lane_group, LANES), 1)
    return jnp.concatenate([both, jnp.zeros((NVEC, LANES), jnp.float32)], axis=0)


def split_out(all_ref, field_ref, search_ref, theta_ref):
    field_ref[...] = all_ref[0:NVEC, 0:QUARTER]
    search_ref[...] = all_ref[NVEC : 2 * NVEC, 0:QUARTER]
    theta_ref[...] = all_ref[48:50, 0:NVEC]


def body(tiles, energy, vectors, previous, coefs, irrep_of_unit, coupled):
    f32 = jnp.float32
    dma = pltpu.SemaphoreType.DMA
    vmem = pl.BlockSpec(memory_space=pltpu.VMEM)
    smem = pl.BlockSpec(memory_space=pltpu.SMEM)
    piece = (GROUP, LANES)
    everything = pl.pallas_call(
        kernel,
        out_shape=jax.ShapeDtypeStruct((56, LANES), f32),
        in_specs=[pl.BlockSpec(memory_space=pl.ANY), vmem, vmem, vmem, vmem, smem, smem],
        out_specs=vmem,
        scratch_shapes=[
            pltpu.VMEM((SEG, 2, SEG), jnp.bfloat16),
            pltpu.VMEM((2, SEG, SEG), jnp.bfloat16),
            pltpu.VMEM((40, LANES), f32),
            pltpu.VMEM((2, LANES, LANES), f32),
            pltpu.VMEM((1, LANES), f32),
            pltpu.VMEM((GROUP, 1, LANES), f32),
            pltpu.VMEM(piece, f32),
            pltpu.VMEM(piece, f32),
            pltpu.VMEM((GROUP, *piece), f32),
            pltpu.VMEM((GROUP, *piece), f32),
            pltpu.VMEM((2, 3, NVEC, SEG), f32),
            pltpu.VMEM((COLS, *piece), f32),
            pltpu.VMEM((2, COLS, *piece), f32),
            pltpu.VMEM((COLS, *piece), f32),
            pltpu.VMEM((2, COLS, *piece), f32),
            pltpu.VMEM((COLS, *piece), f32),
            pltpu.VMEM((2, COLS, *piece), f32),
            pltpu.VMEM((GROUP, *piece), f32),
            pltpu.VMEM((2, COLS, *piece), f32),
            pltpu.VMEM((2, 2, COLS, *piece), f32),
            pltpu.VMEM((COLS + ROWS, *piece), f32),
            pltpu.VMEM((COLS + ROWS, *piece), f32),
            pltpu.VMEM(piece, f32),
            pltpu.VMEM(piece, f32),
            pltpu.VMEM((2, 2, *piece), f32),
            pltpu.VMEM((2, COLS, *piece), f32),
            pltpu.VMEM((2, ROWS, *piece), f32),
            dma, dma, dma,
            dma((2,)), dma((2,)), dma((2,)), dma((2,)), dma((2,)), dma((2,)), dma, dma,
            dma((2, 2)), dma((2,)), dma((2, 2)), dma((2, 2)),
        ],
        compiler_params=pltpu.CompilerParams(collective_id=0, has_side_effects=True),
        name="lobpcg",
    )(tiles, energy[None, :], vectors, previous, coefs, irrep_of_unit, coupled)
    return pl.pallas_call(
        split_out,
        out_shape=(
            jax.ShapeDtypeStruct((NVEC, QUARTER), f32),
            jax.ShapeDtypeStruct((NVEC, QUARTER), f32),
            jax.ShapeDtypeStruct((2, NVEC), f32),
        ),
        in_specs=[vmem],
        out_specs=(vmem, vmem, vmem),
        name="split",
    )(everything)


def solution(mesh):
    placed = (
        P("row", None, "col"),
        P(("row", "col")),
        P(None, ("row", "col")),
        P(None, ("row", "col")),
        P(),
        P(),
        P(),
    )
    return jax.shard_map(
        body,
        mesh=mesh,
        in_specs=placed,
        out_specs=(P(None, ("row", "col")), P(None, ("row", "col")), P()),
        check_vma=False,
    )
```

```python
import jax
import jax.numpy as jnp
from jax import lax
from jax.experimental import pallas as pl
from jax.experimental.pallas import tpu as pltpu
from jax.sharding import PartitionSpec as P

MESH = pl.DeviceIdType.MESH
UNIT = 64
ROWS = 32
COLS = 16
SEG = 512
NVEC = 16
LANES = 128
GROUP = 4
QUARTER = LANES // GROUP
TINY = 1e-37


def remote(src, dst, send, recv, row, col):
    return pltpu.make_async_remote_copy(
        src_ref=src, dst_ref=dst, send_sem=send, recv_sem=recv, device_id=(row, col), device_id_type=MESH
    )


def wait_all(ref, sem):
    pltpu.make_async_copy(ref, ref, sem).wait()


def lane_block():
    return lax.broadcasted_iota(jnp.int32, (NVEC, LANES), 1) // QUARTER


def swapped(parts):
    block = lane_block()
    results = []
    for o in range(GROUP):
        total = None
        for i in range(GROUP):
            part = pltpu.roll(parts[i], QUARTER * ((i - o) % GROUP), 1) if i != o else parts[i]
            total = part if total is None else jnp.where(block == i, part, total)
        results.append(total)
    return results


def unpacked(ref, start=0):
    take = slice(start, start + GROUP)
    parts = [jnp.concatenate([ref[4 * t + g, take] for t in range(GROUP)], axis=0) for g in range(GROUP)]
    rows = swapped(parts)
    tiles = []
    for t in range(GROUP):
        tiles.append(jnp.concatenate([rows[b][4 * t : 4 * t + 4] for b in range(GROUP)], axis=0))
    return jnp.concatenate(tiles, axis=1)


def store_packed(ref, value):
    parts = []
    for b in range(GROUP):
        rows = [value[4 * b : 4 * b + 4, LANES * t : LANES * (t + 1)] for t in range(GROUP)]
        parts.append(jnp.concatenate(rows, axis=0))
    pieces = swapped(parts)
    for t in range(GROUP):
        for g in range(GROUP):
            ref[4 * t + g] = pieces[g][4 * t : 4 * t + 4]


def pack_own(value):
    total = value[0:4]
    for b in range(1, GROUP):
        total = total + pltpu.roll(value[4 * b : 4 * b + 4], QUARTER * b, 1)
    return total


def unpack_own(piece):
    rows = [piece] + [pltpu.roll(piece, LANES - QUARTER * b, 1) for b in range(1, GROUP)]
    return jnp.where(lane_block() == 0, jnp.concatenate(rows, axis=0), 0.0)


def mixed(mix, parts):
    totals = []
    for place, part in parts:
        total = None
        for k in range(NVEC):
            column = mix[:, NVEC * place + k : NVEC * place + k + 1]
            term = column * part[k : k + 1, :]
            total = term if total is None else total + term
        totals.append(total)
    result = totals[0]
    for total in totals[1:]:
        result = result + total
    return result


def kernel(
    tiles_hbm, energy_hbm, vectors_hbm, previous_hbm, coefs_hbm, irrep_hbm, coupled_hbm,
    out_ref,
    vectors_ref, previous_ref, energy_ref, coefs_ref, irrep_ref, coupled_ref, tiles_buf, masked, pad, mix_ref, field_out, image_out,
    field_row, field_col, image_row, image_col,
    direct_out, mirror_out, sums, stat_out, near_stats, far_stats,
    tiles_sem, load_sem, vec_send, vec_recv, sums_send, sums_recv, stat_send, stat_recv,
):
    row = lax.axis_index("row")
    col = lax.axis_index("col")
    home = lax.rem(row, COLS)
    half = row // COLS
    on_diag = home == col
    low = row // 8
    y = lax.rem(row, 8)
    inner = lax.rem(col, 8)
    core = lax.rem(col, 2)
    depth = (col // 8) * 4 + low

    def near_peer(k):
        z = k // 2
        return lax.rem(z, 4) * 8 + y, (z // 4) * 8 + (inner // 2) * 2 + lax.rem(k, 2)

    def far_peer(k):
        return low * 8 + lax.rem(k, 8), (col // 8) * 8 + (k // 8) * 2 + core

    def is_self(r, c):
        return jnp.logical_and(r == row, c == col)

    barrier = pltpu.get_barrier_semaphore()

    def greet(r, c):
        @pl.when(jnp.logical_not(is_self(r, c)))
        def _():
            pl.semaphore_signal(barrier, inc=1, device_id=(r, c), device_id_type=MESH)

    def greet_partners(k, carry):
        greet(lax.rem(k, 2) * COLS + col, k // 2)
        greet(k, home)
        return carry

    def greet_row(k, carry):
        greet(row, k)
        return carry

    lax.fori_loop(0, ROWS, greet_partners, 0)
    lax.fori_loop(0, COLS, greet_row, 0)

    loads = []
    for i, (src, dst) in enumerate((
        (vectors_hbm, vectors_ref), (previous_hbm, previous_ref), (energy_hbm, energy_ref),
        (irrep_hbm, irrep_ref), (coupled_hbm, coupled_ref), (coefs_hbm, coefs_ref),
    )):
        loads.append(pltpu.make_async_copy(src, dst, load_sem.at[i]))
        loads[-1].start()
    load_tiles = pltpu.make_async_copy(tiles_hbm, tiles_buf, tiles_sem)
    load_tiles.start()
    for load in loads:
        load.wait()

    pad[...] = jnp.zeros_like(pad)
    pad[0:16, 0:QUARTER] = vectors_ref[...]
    pad[16:32, 0:QUARTER] = previous_ref[...]
    pad[32:33, 0:QUARTER] = energy_ref[...]
    field_own = pad[0:16]
    search_own = pad[16:32]
    energy = pad[32:33]
    field_out[...] = pack_own(field_own)

    load_tiles.wait()
    strip_sub = lax.broadcasted_iota(jnp.int32, (UNIT, SEG), 0)
    strip_lane = lax.broadcasted_iota(jnp.int32, (UNIT, SEG), 1)
    unit_lane = lax.broadcasted_iota(jnp.int32, (1, SEG), 1) // UNIT

    def mask_strip(i, carry):
        mine = irrep_ref[row * (SEG // UNIT) + i]
        start = pl.multiple_of(i * UNIT, UNIT)
        for h in range(2):
            block = h * COLS + col
            allowed = jnp.zeros((1, SEG), jnp.int32)
            for j in range(SEG // UNIT):
                theirs = irrep_ref[block * (SEG // UNIT) + j]
                allowed = jnp.where(unit_lane == j, coupled_ref[mine, theirs], allowed)
            lower = strip_lane + block * SEG <= strip_sub + (row * SEG + start)
            keep = jnp.logical_and(lower, allowed > 0)
            strip = tiles_buf[pl.ds(start, UNIT), h, :].astype(jnp.float32)
            masked[h, pl.ds(start, UNIT), :] = jnp.where(keep, strip, 0.0).astype(jnp.bfloat16)
        return carry

    lax.fori_loop(0, SEG // UNIT, mask_strip, 0)

    for i in range(2):
        mix_ref[i] = jnp.zeros((LANES, LANES), jnp.float32)
        for j in range(3):
            mix_ref[i, NVEC * j : NVEC * (j + 1), 0:NVEC] = coefs_ref[i, j]
        square = mix_ref[i]
        mix_ref[i] = square.T

    pl.semaphore_wait(barrier, 15 + 64 - 2 * on_diag.astype(jnp.int32))

    def put(src, dst, send, recv, r, c):
        mine = is_self(r, c)

        @pl.when(jnp.logical_not(mine))
        def _():
            remote(src, dst, send, recv, r, c).start()

        @pl.when(mine)
        def _():
            pltpu.make_async_copy(src, dst, recv).start()

    def row_put(src, dst, send, recv):
        def step(k, carry):
            put(src, dst.at[col], send, recv, row, k)
            return carry

        lax.fori_loop(0, COLS, step, 0)

    def col_put(src, dst, send, recv):
        def step(k, carry):
            away = lax.rem(118891828 >> (4 * (k // 4)), 8)
            there = lax.rem(low + lax.rem(k, 4), 4) * 8 + lax.rem(y + away, 8)
            put(src, dst.at[half, col], send, recv, there, home)
            return carry

        lax.fori_loop(0, ROWS, step, 0)

    row_put(field_out, field_row, vec_send.at[0, 1], vec_recv.at[0, 1])
    col_put(field_out, field_col, vec_send.at[0, 0], vec_recv.at[0, 0])
    image_out[GROUP:] = pack_own(mixed(mix_ref[0, 0:NVEC], [(0, field_own), (2, search_own)]))
    energy_part = pack_own(energy * field_own)

    def mirror_products(vectors, which):
        narrow = vectors.astype(jnp.bfloat16)
        for h in range(2):
            mirror = jnp.dot(narrow, masked[h], preferred_element_type=jnp.float32)
            store_packed(mirror_out.at[which, h], mirror)

            def mirror_put(k, carry):
                j = lax.rem(k + row, COLS)
                put(mirror_out.at[which, h, j], sums.at[which, COLS + row], sums_send.at[which, 0], sums_recv.at[which], COLS * h + col, j)
                return carry

            lax.fori_loop(0, COLS, mirror_put, 0)

    def direct_products(vectors, which):
        direct = jnp.zeros((NVEC, SEG), jnp.float32)
        for h in range(2):
            narrow = vectors[h].astype(jnp.bfloat16)
            direct = direct + lax.dot_general(
                narrow, masked[h], (((1,), (1,)), ((), ())), preferred_element_type=jnp.float32
            )
        store_packed(direct_out.at[which], direct)

        def direct_put(k, carry):
            j = lax.rem(k + col, COLS)
            put(direct_out.at[which, j], sums.at[which, col], sums_send.at[which, 1], sums_recv.at[which], row, j)
            return carry

        lax.fori_loop(0, COLS, direct_put, 0)

    def summed(which):
        buf = sums.at[which]
        wait_all(buf, sums_recv.at[which])
        return jnp.sum(buf[...], axis=0)

    sub = lax.broadcasted_iota(jnp.int32, (NVEC, LANES), 0)
    lane = lax.broadcasted_iota(jnp.int32, (NVEC, LANES), 1)
    eye = sub == lane

    def to_column(lanes):
        return jnp.sum(jnp.where(eye, lanes, 0.0), axis=1, keepdims=True)

    def quotient(cross, self_dot):
        usable = self_dot > TINY
        return jnp.where(usable, cross / jnp.where(usable, self_dot, 1.0), 0.0)

    def send_stats(rows, which, hop):
        for i, value in enumerate(rows):
            stat_out[which, hop, i : i + 1, :] = value
        src = stat_out.at[which, hop]

        def near_step(k, carry):
            put(src, near_stats.at[which, depth * 2 + core], stat_send.at[which, 0], stat_recv.at[which, 0], *near_peer(k))
            return carry

        def far_step(k, carry):
            put(src, far_stats.at[which, (inner // 2) * 8 + y], stat_send.at[which, 1], stat_recv.at[which, 1], *far_peer(k))
            return carry

        if hop == 0:
            lax.fori_loop(0, COLS, near_step, 0)
        else:
            lax.fori_loop(0, ROWS, far_step, 0)

    def share_stats(field, image, which):
        self_dot = jnp.sum(field * field, axis=1, keepdims=True)
        cross = jnp.sum(field * image, axis=1, keepdims=True)
        local = quotient(cross, self_dot)
        left = image - local * field
        spread = jnp.sum(left * left, axis=1, keepdims=True)
        rows = [
            jnp.sum(jnp.where(eye, value, 0.0), axis=0, keepdims=True)
            for value in (self_dot, cross, spread, local)
        ]
        send_stats(rows, which, 0)

    def merged(buf):
        self_i, cross_i, spread_i, local_i = [buf[:, i, :] for i in range(4)]
        self_dot = jnp.sum(self_i, axis=0, keepdims=True)
        cross = jnp.sum(cross_i, axis=0, keepdims=True)
        return self_i, spread_i, local_i, self_dot, cross

    def spread_about(self_i, spread_i, local_i, theta):
        away = local_i - theta
        return jnp.sum(spread_i + self_i * away * away, axis=0, keepdims=True)

    def relay_stats(which):
        buf = near_stats.at[which]
        wait_all(buf, stat_recv.at[which, 0])
        self_i, spread_i, local_i, self_dot, cross = merged(buf)
        local = quotient(cross, self_dot)
        send_stats([self_dot, cross, spread_about(self_i, spread_i, local_i, local), local], which, 1)

    def merge_stats(which):
        buf = far_stats.at[which]
        wait_all(buf, stat_recv.at[which, 1])
        self_i, spread_i, local_i, self_dot, cross = merged(buf)
        theta = cross / jnp.where(lane[0:1] < NVEC, self_dot, 1.0)
        spread = spread_about(self_i, spread_i, local_i, theta)
        scale = lax.rsqrt(spread / (ROWS * SEG) + 1e-06)
        out_ref[32 + which : 33 + which, :] = theta
        return to_column(theta), to_column(scale)

    wait_all(field_row, vec_recv.at[0, 1])
    field_r = unpacked(field_row)
    mirror_products(field_r, 0)
    wait_all(field_col, vec_recv.at[0, 0])
    field_c = [unpacked(field_col.at[h]) for h in range(2)]
    direct_products(field_c, 0)
    image_p = summed(0) + energy_part
    image_out[0:GROUP] = image_p
    image_own = unpack_own(image_p)
    share_stats(field_own, image_own, 0)
    row_put(image_out, image_row, vec_send.at[1, 1], vec_recv.at[1, 1])
    col_put(image_out, image_col, vec_send.at[1, 0], vec_recv.at[1, 0])
    relay_stats(0)
    wait_all(image_row, vec_recv.at[1, 1])
    wait_all(image_col, vec_recv.at[1, 0])

    image_r, ready_r = unpacked(image_row), unpacked(image_row, GROUP)
    image_c = [unpacked(image_col.at[h]) for h in range(2)]
    ready_c = [unpacked(image_col.at[h], GROUP) for h in range(2)]
    theta, scale = merge_stats(0)
    mix = [mix_ref[i, 0:NVEC] for i in range(2)]

    def following(field, image, ready):
        scaled = (image - theta * field) * scale
        return ready + mixed(mix[0], [(1, scaled)])

    mirror_products(following(field_r, image_r, ready_r), 1)
    direct_products([following(field_c[h], image_c[h], ready_c[h]) for h in range(2)], 1)
    scaled = (image_own - theta * field_own) * scale
    search_own = mixed(mix[0], [(1, scaled), (2, search_own)])
    field_own = mixed(mix[0], [(0, field_own)]) + search_own
    image_own = unpack_own(summed(1)) + energy * field_own
    share_stats(field_own, image_own, 1)
    search_part = mixed(mix[1], [(2, search_own)])
    field_part = mixed(mix[1], [(0, field_own)])
    relay_stats(1)
    theta, scale = merge_stats(1)
    scaled = (image_own - theta * field_own) * scale
    search_own = search_part + mixed(mix[1], [(1, scaled)])
    out_ref[0:NVEC, :] = field_part + search_own
    out_ref[NVEC : 2 * NVEC, :] = search_own

    def drain(sem, ref, whole, diagonal):
        if not diagonal:
            wait_all(ref.at[pl.ds(0, whole)], sem)
        else:
            @pl.when(on_diag)
            def _():
                wait_all(ref.at[pl.ds(0, whole - 1)], sem)

            @pl.when(jnp.logical_not(on_diag))
            def _():
                wait_all(ref.at[pl.ds(0, whole)], sem)

    def drain_wide():
        wait_all(image_col.at[0], vec_send.at[1, 0])

        @pl.when(on_diag)
        def _():
            wait_all(image_col.at[1, pl.ds(0, COLS - 1)], vec_send.at[1, 0])

        @pl.when(jnp.logical_not(on_diag))
        def _():
            wait_all(image_col.at[1], vec_send.at[1, 0])

    spare = sums.at[0]
    drain(vec_send.at[0, 0], spare, ROWS, True)
    drain(vec_send.at[0, 1], spare, COLS - 1, False)
    wide = image_col.at[0]
    drain(vec_send.at[1, 1], wide, COLS - 1, False)
    drain_wide()
    for which in range(2):
        drain(sums_send.at[which, 0], spare, 2 * COLS, True)
        drain(sums_send.at[which, 1], spare, COLS - 1, False)
    for which in range(2):
        drain(stat_send.at[which, 0], spare, COLS - 1, False)
        drain(stat_send.at[which, 1], spare, ROWS - 1, False)


def split_out(all_ref, field_ref, search_ref, theta_ref):
    field_ref[...] = all_ref[0:NVEC, 0:QUARTER]
    search_ref[...] = all_ref[NVEC : 2 * NVEC, 0:QUARTER]
    theta_ref[...] = all_ref[32:34, 0:NVEC]


def body(tiles, energy, vectors, previous, coefs, irrep_of_unit, coupled):
    f32 = jnp.float32
    dma = pltpu.SemaphoreType.DMA
    vmem = pl.BlockSpec(memory_space=pltpu.VMEM)
    piece = (GROUP, LANES)
    everything = pl.pallas_call(
        kernel,
        out_shape=jax.ShapeDtypeStruct((40, LANES), f32),
        in_specs=[pl.BlockSpec(memory_space=pl.ANY)] * 7,
        out_specs=vmem,
        scratch_shapes=[
            pltpu.VMEM((NVEC, QUARTER), f32),
            pltpu.VMEM((NVEC, QUARTER), f32),
            pltpu.VMEM((1, QUARTER), f32),
            pltpu.VMEM(coefs.shape, f32),
            pltpu.SMEM(irrep_of_unit.shape, jnp.int32),
            pltpu.SMEM(coupled.shape, jnp.int32),
            pltpu.VMEM((SEG, 2, SEG), jnp.bfloat16),
            pltpu.VMEM((2, SEG, SEG), jnp.bfloat16),
            pltpu.VMEM((40, LANES), f32),
            pltpu.VMEM((2, LANES, LANES), f32),
            pltpu.VMEM(piece, f32),
            pltpu.VMEM((2 * GROUP, LANES), f32),
            pltpu.VMEM((COLS, *piece), f32),
            pltpu.VMEM((2, COLS, *piece), f32),
            pltpu.VMEM((COLS, 2 * GROUP, LANES), f32),
            pltpu.VMEM((2, COLS, 2 * GROUP, LANES), f32),
            pltpu.VMEM((2, COLS, *piece), f32),
            pltpu.VMEM((2, 2, COLS, *piece), f32),
            pltpu.VMEM((2, COLS + ROWS, *piece), f32),
            pltpu.VMEM((2, 2, *piece), f32),
            pltpu.VMEM((2, COLS, *piece), f32),
            pltpu.VMEM((2, ROWS, *piece), f32),
            dma,
            dma((6,)), dma((2, 2)), dma((2, 2)), dma((2, 2)), dma((2,)), dma((2, 2)), dma((2, 2)),
        ],
        compiler_params=pltpu.CompilerParams(collective_id=0, has_side_effects=True),
        name="lobpcg",
    )(tiles, energy[None, :], vectors, previous, coefs, irrep_of_unit, coupled)
    return pl.pallas_call(
        split_out,
        out_shape=(
            jax.ShapeDtypeStruct((NVEC, QUARTER), f32),
            jax.ShapeDtypeStruct((NVEC, QUARTER), f32),
            jax.ShapeDtypeStruct((2, NVEC), f32),
        ),
        in_specs=[vmem],
        out_specs=(vmem, vmem, vmem),
        name="split",
    )(everything)


def solution(mesh):
    placed = (
        P("row", None, "col"),
        P(("row", "col")),
        P(None, ("row", "col")),
        P(None, ("row", "col")),
        P(),
        P(),
        P(),
    )
    return jax.shard_map(
        body,
        mesh=mesh,
        in_specs=placed,
        out_specs=(P(None, ("row", "col")), P(None, ("row", "col")), P()),
        check_vma=False,
    )
```

```python
import jax
import jax.numpy as jnp
from jax import lax
from jax.experimental import pallas as pl
from jax.experimental.pallas import tpu as pltpu
from jax.sharding import PartitionSpec as P

MESH = pl.DeviceIdType.MESH
UNIT = 64
ROWS = 32
COLS = 16
SEG = 512
NVEC = 16
LANES = 128
GROUP = 4
QUARTER = LANES // GROUP
TINY = 1e-37


def remote(src, dst, send, recv, row, col):
    return pltpu.make_async_remote_copy(
        src_ref=src, dst_ref=dst, send_sem=send, recv_sem=recv, device_id=(row, col), device_id_type=MESH
    )


def wait_all(ref, sem):
    pltpu.make_async_copy(ref, ref, sem).wait()


def lane_block():
    return lax.broadcasted_iota(jnp.int32, (NVEC, LANES), 1) // QUARTER


def swapped(parts):
    block = lane_block()
    results = []
    for o in range(GROUP):
        total = None
        for i in range(GROUP):
            part = pltpu.roll(parts[i], QUARTER * ((i - o) % GROUP), 1) if i != o else parts[i]
            total = part if total is None else jnp.where(block == i, part, total)
        results.append(total)
    return results


def unpacked(ref, start=0):
    take = slice(start, start + GROUP)
    parts = [jnp.concatenate([ref[4 * t + g, take] for t in range(GROUP)], axis=0) for g in range(GROUP)]
    rows = swapped(parts)
    tiles = []
    for t in range(GROUP):
        tiles.append(jnp.concatenate([rows[b][4 * t : 4 * t + 4] for b in range(GROUP)], axis=0))
    return jnp.concatenate(tiles, axis=1)


def store_packed(ref, value):
    parts = []
    for b in range(GROUP):
        rows = [value[4 * b : 4 * b + 4, LANES * t : LANES * (t + 1)] for t in range(GROUP)]
        parts.append(jnp.concatenate(rows, axis=0))
    pieces = swapped(parts)
    for t in range(GROUP):
        for g in range(GROUP):
            ref[4 * t + g] = pieces[g][4 * t : 4 * t + 4]


def pack_own(value):
    total = value[0:4]
    for b in range(1, GROUP):
        total = total + pltpu.roll(value[4 * b : 4 * b + 4], QUARTER * b, 1)
    return total


def unpack_own(piece):
    rows = [piece] + [pltpu.roll(piece, LANES - QUARTER * b, 1) for b in range(1, GROUP)]
    return jnp.where(lane_block() == 0, jnp.concatenate(rows, axis=0), 0.0)


def mixed(mix, parts):
    totals = []
    for place, part in parts:
        total = None
        for k in range(NVEC):
            column = mix[:, NVEC * place + k : NVEC * place + k + 1]
            term = column * part[k : k + 1, :]
            total = term if total is None else total + term
        totals.append(total)
    result = totals[0]
    for total in totals[1:]:
        result = result + total
    return result


def kernel(
    tiles_hbm, energy_hbm, vectors_hbm, previous_hbm, coefs_hbm, irrep_hbm, coupled_hbm,
    out_ref,
    vectors_ref, previous_ref, energy_ref, coefs_ref, irrep_ref, coupled_ref, tiles_buf, masked, pad, mix_ref, field_out, image_out,
    field_row, field_col, image_row, image_col,
    direct_out, mirror_out, sums, stat_out, near_stats, far_stats,
    tiles_sem, load_sem, vec_send, vec_recv, sums_send, sums_recv, stat_send, stat_recv,
):
    row = lax.axis_index("row")
    col = lax.axis_index("col")
    home = lax.rem(row, COLS)
    half = row // COLS
    on_diag = home == col
    low = row // 8
    y = lax.rem(row, 8)
    inner = lax.rem(col, 8)
    core = lax.rem(col, 2)
    depth = (col // 8) * 4 + low

    def near_peer(k):
        z = k // 2
        return lax.rem(z, 4) * 8 + y, (z // 4) * 8 + (inner // 2) * 2 + lax.rem(k, 2)

    def far_peer(k):
        return low * 8 + lax.rem(k, 8), (col // 8) * 8 + (k // 8) * 2 + core

    def is_self(r, c):
        return jnp.logical_and(r == row, c == col)

    barrier = pltpu.get_barrier_semaphore()

    def greet(r, c):
        @pl.when(jnp.logical_not(is_self(r, c)))
        def _():
            pl.semaphore_signal(barrier, inc=1, device_id=(r, c), device_id_type=MESH)

    def greet_sources(k, carry):
        greet(lax.rem(k, 2) * COLS + col, 2 * (k // 2))
        return carry

    def greet_row(k, carry):
        greet(row, 2 * k)
        return carry

    lax.fori_loop(0, COLS, greet_sources, 0)
    lax.fori_loop(0, COLS // 2, greet_row, 0)

    loads = []
    for i, (src, dst) in enumerate((
        (vectors_hbm, vectors_ref), (previous_hbm, previous_ref), (energy_hbm, energy_ref),
        (irrep_hbm, irrep_ref), (coupled_hbm, coupled_ref), (coefs_hbm, coefs_ref),
    )):
        loads.append(pltpu.make_async_copy(src, dst, load_sem.at[i]))
        loads[-1].start()
    load_tiles = pltpu.make_async_copy(tiles_hbm, tiles_buf, tiles_sem)
    load_tiles.start()
    for load in loads:
        load.wait()

    pad[...] = jnp.zeros_like(pad)
    pad[0:16, 0:QUARTER] = vectors_ref[...]
    pad[16:32, 0:QUARTER] = previous_ref[...]
    pad[32:33, 0:QUARTER] = energy_ref[...]
    field_own = pad[0:16]
    search_own = pad[16:32]
    energy = pad[32:33]
    field_out[...] = pack_own(field_own)

    load_tiles.wait()
    strip_sub = lax.broadcasted_iota(jnp.int32, (UNIT, SEG), 0)
    strip_lane = lax.broadcasted_iota(jnp.int32, (UNIT, SEG), 1)
    unit_lane = lax.broadcasted_iota(jnp.int32, (1, SEG), 1) // UNIT

    def mask_strip(i, carry):
        mine = irrep_ref[row * (SEG // UNIT) + i]
        start = pl.multiple_of(i * UNIT, UNIT)
        for h in range(2):
            block = h * COLS + col
            allowed = jnp.zeros((1, SEG), jnp.int32)
            for j in range(SEG // UNIT):
                theirs = irrep_ref[block * (SEG // UNIT) + j]
                allowed = jnp.where(unit_lane == j, coupled_ref[mine, theirs], allowed)
            lower = strip_lane + block * SEG <= strip_sub + (row * SEG + start)
            keep = jnp.logical_and(lower, allowed > 0)
            strip = tiles_buf[pl.ds(start, UNIT), h, :].astype(jnp.float32)
            masked[h, pl.ds(start, UNIT), :] = jnp.where(keep, strip, 0.0).astype(jnp.bfloat16)
        return carry

    lax.fori_loop(0, SEG // UNIT, mask_strip, 0)

    for i in range(2):
        mix_ref[i] = jnp.zeros((LANES, LANES), jnp.float32)
        for j in range(3):
            mix_ref[i, NVEC * j : NVEC * (j + 1), 0:NVEC] = coefs_ref[i, j]
        square = mix_ref[i]
        mix_ref[i] = square.T

    first = core == 0
    skipped = jnp.logical_and(on_diag, first).astype(jnp.int32)

    @pl.when(first)
    def _():
        pl.semaphore_wait(barrier, 15 + 32 - skipped)
        pl.semaphore_signal(barrier, inc=1, device_id=(row, col + 1), device_id_type=MESH)

    @pl.when(jnp.logical_not(first))
    def _():
        pl.semaphore_wait(barrier, 1)

    def put(src, dst, send, recv, r, c):
        mine = is_self(r, c)

        @pl.when(jnp.logical_not(mine))
        def _():
            remote(src, dst, send, recv, r, c).start()

        @pl.when(mine)
        def _():
            pltpu.make_async_copy(src, dst, recv).start()

    def row_put(src, dst, send, recv):
        def step(k, carry):
            put(src, dst.at[col], send, recv, row, k)
            return carry

        lax.fori_loop(0, COLS, step, 0)

    def col_put(src, dst, send, recv):
        def step(k, carry):
            away = lax.rem(118891828 >> (4 * (k // 4)), 8)
            there = lax.rem(low + lax.rem(k, 4), 4) * 8 + lax.rem(y + away, 8)
            put(src, dst.at[half, col], send, recv, there, home)
            return carry

        lax.fori_loop(0, ROWS, step, 0)

    row_put(field_out, field_row, vec_send.at[0, 1], vec_recv.at[0, 1])
    col_put(field_out, field_col, vec_send.at[0, 0], vec_recv.at[0, 0])
    image_out[GROUP:] = pack_own(mixed(mix_ref[0, 0:NVEC], [(0, field_own), (2, search_own)]))
    energy_part = pack_own(energy * field_own)

    def mirror_products(vectors, which, first=None):
        narrow = vectors.astype(jnp.bfloat16)
        for h in range(2):
            mirror = jnp.dot(narrow, masked[h], preferred_element_type=jnp.float32)
            store_packed(mirror_out.at[which, h], mirror)

        if first is not None:
            first()

        def mirror_put(k, carry):
            h = k // COLS
            j = lax.rem(k + row, COLS)
            put(mirror_out.at[which, h, j], sums.at[which, COLS + row], sums_send.at[which, 0], sums_recv.at[which], COLS * h + col, j)
            return carry

        lax.fori_loop(0, 2 * COLS, mirror_put, 0)

    def direct_products(vectors, which):
        direct = jnp.zeros((NVEC, SEG), jnp.float32)
        for h in range(2):
            narrow = vectors[h].astype(jnp.bfloat16)
            direct = direct + lax.dot_general(
                narrow, masked[h], (((1,), (1,)), ((), ())), preferred_element_type=jnp.float32
            )
        store_packed(direct_out.at[which], direct)

        def direct_put(k, carry):
            j = lax.rem(k + col, COLS)
            put(direct_out.at[which, j], sums.at[which, col], sums_send.at[which, 1], sums_recv.at[which], row, j)
            return carry

        lax.fori_loop(0, COLS, direct_put, 0)

    def summed(which):
        buf = sums.at[which]
        wait_all(buf, sums_recv.at[which])
        return jnp.sum(buf[...], axis=0)

    sub = lax.broadcasted_iota(jnp.int32, (NVEC, LANES), 0)
    lane = lax.broadcasted_iota(jnp.int32, (NVEC, LANES), 1)
    eye = sub == lane

    def to_column(lanes):
        return jnp.sum(jnp.where(eye, lanes, 0.0), axis=1, keepdims=True)

    def quotient(cross, self_dot):
        usable = self_dot > TINY
        return jnp.where(usable, cross / jnp.where(usable, self_dot, 1.0), 0.0)

    def send_stats(rows, which, hop):
        for i, value in enumerate(rows):
            stat_out[which, hop, i : i + 1, :] = value
        src = stat_out.at[which, hop]

        def near_step(k, carry):
            put(src, near_stats.at[which, depth * 2 + core], stat_send.at[which, 0], stat_recv.at[which, 0], *near_peer(k))
            return carry

        def far_step(k, carry):
            put(src, far_stats.at[which, (inner // 2) * 8 + y], stat_send.at[which, 1], stat_recv.at[which, 1], *far_peer(k))
            return carry

        if hop == 0:
            lax.fori_loop(0, COLS, near_step, 0)
        else:
            lax.fori_loop(0, ROWS, far_step, 0)

    def share_stats(field, image, which):
        self_dot = jnp.sum(field * field, axis=1, keepdims=True)
        cross = jnp.sum(field * image, axis=1, keepdims=True)
        local = quotient(cross, self_dot)
        left = image - local * field
        spread = jnp.sum(left * left, axis=1, keepdims=True)
        rows = [
            jnp.sum(jnp.where(eye, value, 0.0), axis=0, keepdims=True)
            for value in (self_dot, cross, spread, local)
        ]
        send_stats(rows, which, 0)

    def merged(buf):
        self_i, cross_i, spread_i, local_i = [buf[:, i, :] for i in range(4)]
        self_dot = jnp.sum(self_i, axis=0, keepdims=True)
        cross = jnp.sum(cross_i, axis=0, keepdims=True)
        return self_i, spread_i, local_i, self_dot, cross

    def spread_about(self_i, spread_i, local_i, theta):
        away = local_i - theta
        return jnp.sum(spread_i + self_i * away * away, axis=0, keepdims=True)

    def relay_stats(which):
        buf = near_stats.at[which]
        wait_all(buf, stat_recv.at[which, 0])
        self_i, spread_i, local_i, self_dot, cross = merged(buf)
        local = quotient(cross, self_dot)
        send_stats([self_dot, cross, spread_about(self_i, spread_i, local_i, local), local], which, 1)

    def merge_stats(which):
        buf = far_stats.at[which]
        wait_all(buf, stat_recv.at[which, 1])
        self_i, spread_i, local_i, self_dot, cross = merged(buf)
        theta = cross / jnp.where(lane[0:1] < NVEC, self_dot, 1.0)
        spread = spread_about(self_i, spread_i, local_i, theta)
        scale = lax.rsqrt(spread / (ROWS * SEG) + 1e-06)
        out_ref[32 + which : 33 + which, :] = theta
        return to_column(theta), to_column(scale)

    wait_all(field_row, vec_recv.at[0, 1])
    field_r = unpacked(field_row)
    mirror_products(field_r, 0, lambda: wait_all(field_col, vec_recv.at[0, 0]))
    field_c = [unpacked(field_col.at[h]) for h in range(2)]
    direct_products(field_c, 0)
    image_p = summed(0) + energy_part
    image_out[0:GROUP] = image_p
    image_own = unpack_own(image_p)
    share_stats(field_own, image_own, 0)
    row_put(image_out, image_row, vec_send.at[1, 1], vec_recv.at[1, 1])
    col_put(image_out, image_col, vec_send.at[1, 0], vec_recv.at[1, 0])
    relay_stats(0)
    wait_all(image_row, vec_recv.at[1, 1])
    wait_all(image_col, vec_recv.at[1, 0])

    image_r, ready_r = unpacked(image_row), unpacked(image_row, GROUP)
    image_c = [unpacked(image_col.at[h]) for h in range(2)]
    ready_c = [unpacked(image_col.at[h], GROUP) for h in range(2)]
    theta, scale = merge_stats(0)
    mix = [mix_ref[i, 0:NVEC] for i in range(2)]

    def following(field, image, ready):
        scaled = (image - theta * field) * scale
        return ready + mixed(mix[0], [(1, scaled)])

    mirror_products(following(field_r, image_r, ready_r), 1)
    direct_products([following(field_c[h], image_c[h], ready_c[h]) for h in range(2)], 1)
    scaled = (image_own - theta * field_own) * scale
    search_own = mixed(mix[0], [(1, scaled), (2, search_own)])
    field_own = mixed(mix[0], [(0, field_own)]) + search_own
    image_own = unpack_own(summed(1)) + energy * field_own
    share_stats(field_own, image_own, 1)
    search_part = mixed(mix[1], [(2, search_own)])
    field_part = mixed(mix[1], [(0, field_own)])
    relay_stats(1)
    theta, scale = merge_stats(1)
    scaled = (image_own - theta * field_own) * scale
    search_own = search_part + mixed(mix[1], [(1, scaled)])
    out_ref[0:NVEC, :] = field_part + search_own
    out_ref[NVEC : 2 * NVEC, :] = search_own

    def drain(sem, ref, whole, diagonal):
        if not diagonal:
            wait_all(ref.at[pl.ds(0, whole)], sem)
        else:
            @pl.when(on_diag)
            def _():
                wait_all(ref.at[pl.ds(0, whole - 1)], sem)

            @pl.when(jnp.logical_not(on_diag))
            def _():
                wait_all(ref.at[pl.ds(0, whole)], sem)

    def drain_wide():
        wait_all(image_col.at[0], vec_send.at[1, 0])

        @pl.when(on_diag)
        def _():
            wait_all(image_col.at[1, pl.ds(0, COLS - 1)], vec_send.at[1, 0])

        @pl.when(jnp.logical_not(on_diag))
        def _():
            wait_all(image_col.at[1], vec_send.at[1, 0])

    spare = sums.at[0]
    drain(vec_send.at[0, 0], spare, ROWS, True)
    drain(vec_send.at[0, 1], spare, COLS - 1, False)
    wide = image_col.at[0]
    drain(vec_send.at[1, 1], wide, COLS - 1, False)
    drain_wide()
    for which in range(2):
        drain(sums_send.at[which, 0], spare, 2 * COLS, True)
        drain(sums_send.at[which, 1], spare, COLS - 1, False)
    for which in range(2):
        drain(stat_send.at[which, 0], spare, COLS - 1, False)
        drain(stat_send.at[which, 1], spare, ROWS - 1, False)


def split_out(all_ref, field_ref, search_ref, theta_ref):
    field_ref[...] = all_ref[0:NVEC, 0:QUARTER]
    search_ref[...] = all_ref[NVEC : 2 * NVEC, 0:QUARTER]
    theta_ref[...] = all_ref[32:34, 0:NVEC]


def body(tiles, energy, vectors, previous, coefs, irrep_of_unit, coupled):
    f32 = jnp.float32
    dma = pltpu.SemaphoreType.DMA
    vmem = pl.BlockSpec(memory_space=pltpu.VMEM)
    piece = (GROUP, LANES)
    everything = pl.pallas_call(
        kernel,
        out_shape=jax.ShapeDtypeStruct((40, LANES), f32),
        in_specs=[pl.BlockSpec(memory_space=pl.ANY)] * 7,
        out_specs=vmem,
        scratch_shapes=[
            pltpu.VMEM((NVEC, QUARTER), f32),
            pltpu.VMEM((NVEC, QUARTER), f32),
            pltpu.VMEM((1, QUARTER), f32),
            pltpu.VMEM(coefs.shape, f32),
            pltpu.SMEM(irrep_of_unit.shape, jnp.int32),
            pltpu.SMEM(coupled.shape, jnp.int32),
            pltpu.VMEM((SEG, 2, SEG), jnp.bfloat16),
            pltpu.VMEM((2, SEG, SEG), jnp.bfloat16),
            pltpu.VMEM((40, LANES), f32),
            pltpu.VMEM((2, LANES, LANES), f32),
            pltpu.VMEM(piece, f32),
            pltpu.VMEM((2 * GROUP, LANES), f32),
            pltpu.VMEM((COLS, *piece), f32),
            pltpu.VMEM((2, COLS, *piece), f32),
            pltpu.VMEM((COLS, 2 * GROUP, LANES), f32),
            pltpu.VMEM((2, COLS, 2 * GROUP, LANES), f32),
            pltpu.VMEM((2, COLS, *piece), f32),
            pltpu.VMEM((2, 2, COLS, *piece), f32),
            pltpu.VMEM((2, COLS + ROWS, *piece), f32),
            pltpu.VMEM((2, 2, *piece), f32),
            pltpu.VMEM((2, COLS, *piece), f32),
            pltpu.VMEM((2, ROWS, *piece), f32),
            dma,
            dma((6,)), dma((2, 2)), dma((2, 2)), dma((2, 2)), dma((2,)), dma((2, 2)), dma((2, 2)),
        ],
        compiler_params=pltpu.CompilerParams(collective_id=0, has_side_effects=True),
        name="lobpcg",
    )(tiles, energy[None, :], vectors, previous, coefs, irrep_of_unit, coupled)
    return pl.pallas_call(
        split_out,
        out_shape=(
            jax.ShapeDtypeStruct((NVEC, QUARTER), f32),
            jax.ShapeDtypeStruct((NVEC, QUARTER), f32),
            jax.ShapeDtypeStruct((2, NVEC), f32),
        ),
        in_specs=[vmem],
        out_specs=(vmem, vmem, vmem),
        name="split",
    )(everything)


def solution(mesh):
    placed = (
        P("row", None, "col"),
        P(("row", "col")),
        P(None, ("row", "col")),
        P(None, ("row", "col")),
        P(),
        P(),
        P(),
    )
    return jax.shard_map(
        body,
        mesh=mesh,
        in_specs=placed,
        out_specs=(P(None, ("row", "col")), P(None, ("row", "col")), P()),
        check_vma=False,
    )
```
